512 devices in a mesh: loop: 32 (over z_lo, x, core), grp: 16 (over z_hi, y).
Axes of the slice: x: 4, y: 8, z: 8 (z_hi: 2, z_lo: 4; z = z_hi * 4 + z_lo), core: 2. Of those that a mesh axis runs over, the one named last changes fastest.
Arguments:
- queries: bfloat16 [131072, 512], P(('loop', 'grp')), may hold values from -24 to 24
- key_rows: bfloat16 [131072, 512], P(('loop', 'grp')), may hold values from -4 to 4
- value_rows: bfloat16 [131072, 512], P(('loop', 'grp')), may hold values from -6 to 6
- out_weight: bfloat16 [512, 512], replicated, may hold values from -0.25 to 0.25
- tile_list: int32 [512, 4], P(('loop', 'grp')), may hold values from 0 to 7, as said below
- expander_order: int32 [3, 131072], P(None, ('loop', 'grp')), may hold values from 0 to 255, as said below
- expander_bias: float32 [3, 8], replicated, may hold values from 2 to 6
Outputs:
- layer_output: bfloat16 [131072, 512], P(('loop', 'grp'))
The draws below stay inside these ranges and needn't reach their ends.
Inputs may be any that keep to these rules, and one draw needn't show every extreme that they name: `tile_list`: entry 0 of every row is 3, the partition's own block. Each other entry is 3 + o for a loop offset o with 0 < |o| <= 3, distinct within a row, or the padding value 2 * 3 + 1; every row has at least one non-padding neighbour entry. `expander_order`: for each matching and each partition, the 256 entries of that partition are a permutation of 0 to 255.
All inputs are finite; a program needn't handle non-finite values.
Results may differ from the reference program's by a relative error of at most 0.0075.
Values may be sent and summed in bfloat16 or wider, within the bound.
A program may use at most 128 MiB of HBM per device.

```python
import math
import jax
import jax.numpy as jnp
from jax import lax

HEADS = 8
HEAD = 64
D = 512
ROWS = 256
RADIUS = 3
TILES = 4
MATCHINGS = 3
PARTS_SIZE = 512
NODES = 131072
N_LOOP = 32
N_GRP = 16


def score_base(key):
    base = jax.random.fold_in(key, 1234)
    shape_all = (NODES, HEADS * HEAD)
    drawn_keys = jnp.clip(jax.random.normal(jax.random.fold_in(base, 1), shape_all, jnp.float32), -4.0, 4.0)
    drawn_queries = jnp.clip(jax.random.normal(jax.random.fold_in(base, 2), shape_all, jnp.float32), -4.0, 4.0)
    return (drawn_keys, drawn_queries)


def draw_key_rows(key, part):
    drawn_keys, drawn_queries = score_base(key)
    return drawn_keys.astype(jnp.bfloat16)


def draw_queries(key, part):
    drawn_keys, drawn_queries = score_base(key)
    return drawn_queries.astype(jnp.bfloat16)


def draw_tile_list(key, part):
    base = jax.random.fold_in(key, 77)
    part_keys = jax.random.split(jax.random.fold_in(base, 1), PARTS_SIZE)
    nonzero = jnp.array([value for value in range(2 * RADIUS + 1) if value != RADIUS], jnp.int32)
    shuffled = jax.vmap(lambda one_key: jax.random.permutation(one_key, nonzero))(part_keys)
    counts = jax.random.randint(jax.random.fold_in(base, 2), (PARTS_SIZE,), 1, TILES)
    counts = counts.at[0].set(TILES - 1).at[1].set(1)
    slot_ids = jnp.arange(TILES - 1, dtype=jnp.int32)[None, :]
    chosen = jnp.where(slot_ids < counts[:, None], shuffled[:, :TILES - 1], 2 * RADIUS + 1)
    chosen = chosen.at[0].set(jnp.array([0, 2 * RADIUS, 1], jnp.int32))
    own_block = jnp.full((PARTS_SIZE, 1), RADIUS, jnp.int32)
    return jnp.concatenate([own_block, chosen], axis=1).astype(jnp.int32)


def draw_expander_order(key, part):
    base = jax.random.fold_in(key, 99)
    row_keys = jax.random.split(base, MATCHINGS * PARTS_SIZE)
    shuffled = jax.vmap(lambda one_key: jax.random.permutation(one_key, ROWS))(row_keys)
    return shuffled.reshape(MATCHINGS, PARTS_SIZE * ROWS).astype(jnp.int32)


def block_levels(rng, shape, cuts, smallest, high):
    factor_of = 1.0
    for dim, shards_of in cuts:
        draws = jax.random.uniform(jax.random.fold_in(jax.random.fold_in(rng, 6), dim), (shards_of,), jnp.float32, smallest / len(cuts), high / len(cuts))
        factor_of = factor_of * jnp.repeat(jnp.exp(draws), shape[dim] // shards_of).reshape((-1,) + (1,) * (len(shape) - 1 - dim))
    return factor_of


def normal_values(rng, shape, spread, bound, cuts=(), kind=jnp.bfloat16):
    gain = block_levels(rng, shape, cuts, -0.22, 0.18) if cuts else 1.0
    drawn = jax.random.normal(rng, shape, jnp.float32) * spread * gain
    return jnp.minimum(jnp.maximum(drawn, -bound), bound).astype(kind)


def setup_inputs(seed: int = 0) -> dict:
    arg_keys = jax.random.split(jax.random.key(seed), 8)
    queries = draw_queries(jax.random.fold_in(arg_keys[7], 71), 0)
    key_rows = draw_key_rows(jax.random.fold_in(arg_keys[7], 71), 0)
    value_rows = normal_values(arg_keys[2], (NODES, D), 1.0, 6.0, ((0, 512),))
    out_weight = normal_values(arg_keys[3], (D, D), D ** -0.5, 0.25)
    tile_list = draw_tile_list(jax.random.fold_in(arg_keys[7], 71), 0)
    expander_order = draw_expander_order(jax.random.fold_in(arg_keys[7], 71), 0)
    expander_bias = jnp.clip(jnp.exp(jax.random.uniform(arg_keys[6], (MATCHINGS, HEADS), jnp.float32, math.log(2.0), math.log(6.0))), 2.0, 6.0)
    return dict(queries=queries, key_rows=key_rows, value_rows=value_rows, out_weight=out_weight, tile_list=tile_list, expander_order=expander_order, expander_bias=expander_bias)


NEG_FILL = -1e30


def partner_nodes(expander_order):
    bucket_size = ROWS // N_GRP
    order_table = expander_order.reshape(MATCHINGS, N_LOOP, N_GRP, ROWS)
    position = jnp.argsort(order_table, axis=-1).astype(jnp.int32)
    bucket_id = position // bucket_size
    partner_pos = jnp.where(bucket_id == 0, jnp.bitwise_xor(position, 1), position)
    group_ids = jnp.arange(N_GRP, dtype=jnp.int32)[None, None, :, None]
    partner_grp = jnp.bitwise_xor(group_ids, bucket_id)
    match_ids = jnp.arange(MATCHINGS, dtype=jnp.int32)[:, None, None, None]
    loop_ids = jnp.arange(N_LOOP, dtype=jnp.int32)[None, :, None, None]
    partner_row = order_table[match_ids, loop_ids, partner_grp, partner_pos]
    partner_ids = (loop_ids * N_GRP + partner_grp) * ROWS + partner_row
    return partner_ids.reshape(MATCHINGS, PARTS_SIZE, ROWS).astype(jnp.int32)


def reference(queries, key_rows, value_rows, out_weight, tile_list, expander_order, expander_bias):
    score_scale = HEAD ** -0.5
    partners = partner_nodes(expander_order)
    query_parts = queries.reshape(PARTS_SIZE, ROWS, HEADS, HEAD)
    key_parts = key_rows.reshape(PARTS_SIZE, ROWS, HEADS, HEAD)
    value_parts = value_rows.reshape(PARTS_SIZE, ROWS, HEADS, HEAD)
    key_nodes = key_rows.reshape(NODES, HEADS, HEAD)
    value_nodes = value_rows.reshape(NODES, HEADS, HEAD)

    def one_part(part_index):
        loop_pos = part_index // N_GRP
        grp_pos = part_index % N_GRP
        tiles_here = tile_list[part_index]
        sources = (((loop_pos + tiles_here - RADIUS) % N_LOOP) * N_GRP + grp_pos).astype(jnp.int32)
        tile_valid = tiles_here <= 2 * RADIUS
        block_keys = key_parts[sources].reshape(TILES * ROWS, HEADS, HEAD).astype(jnp.float32)
        block_vals = value_parts[sources].reshape(TILES * ROWS, HEADS, HEAD).astype(jnp.float32)
        query_here = query_parts[part_index].astype(jnp.float32)
        scores = jnp.einsum("rhe,nhe->hrn", query_here, block_keys) * score_scale
        key_mask = jnp.repeat(tile_valid, ROWS)[None, None, :]
        scores = jnp.where(key_mask, scores, NEG_FILL)
        partner_idx = partners[:, part_index]
        partner_keys = key_nodes[partner_idx].astype(jnp.float32)
        partner_vals = value_nodes[partner_idx].astype(jnp.float32)
        expander_scores = jnp.einsum("rhe,jrhe->jrh", query_here, partner_keys) * score_scale + expander_bias[:, None, :]
        row_max = jnp.maximum(jnp.max(scores, axis=-1).T, jnp.max(expander_scores, axis=0))
        weights = jnp.where(key_mask, jnp.exp(scores - row_max.T[:, :, None]), 0.0)
        expander_w = jnp.exp(expander_scores - row_max[None])
        denominator = jnp.sum(weights, axis=-1).T + jnp.sum(expander_w, axis=0)
        weights_low = lax.optimization_barrier(weights.astype(jnp.bfloat16)).astype(jnp.float32)
        expander_low = lax.optimization_barrier(expander_w.astype(jnp.bfloat16)).astype(jnp.float32)
        numerator = jnp.einsum("hrn,nhe->rhe", weights_low, block_vals)
        numerator = numerator + jnp.sum(expander_low[..., None] * partner_vals, axis=0)
        attended = (numerator / denominator[..., None]).reshape(ROWS, HEADS * HEAD).astype(jnp.bfloat16)
        return jnp.dot(attended, out_weight, preferred_element_type=jnp.float32).astype(jnp.bfloat16)

    outputs = lax.map(one_part, jnp.arange(PARTS_SIZE, dtype=jnp.int32))
    return outputs.reshape(NODES, HEADS * HEAD)
```

```python
import jax
import jax.numpy as jnp
from jax import lax
from jax.experimental import pallas as pl
from jax.experimental.pallas import tpu as pltpu
from jax.sharding import PartitionSpec as P

MESH = pl.DeviceIdType.MESH
NEG_FILL = -1e30
RADIUS = 3
BUCKET_ORDER = (15, 1, 8, 2, 14, 3, 9, 4, 13, 5, 10, 6, 12, 7, 11)


def kernel(
    sizes,
    q_hbm,
    k_hbm,
    v_hbm,
    order_hbm,
    tile_hbm,
    bias_hbm,
    att_ref,
    order_ref,
    tile_ref,
    bias_ref,
    tiles,
    q_vmem,
    q_blocks,
    send_buf,
    recv_buf,
    run_max,
    run_sum,
    run_acc,
    acc_rows,
    partner_vals,
    expander_e,
    local_sem,
    tile_send,
    tile_recv,
    exp_send,
    exp_recv,
):
    n_loop, n_grp, matchings, heads, head = sizes
    rows, width = q_vmem.shape
    bucket = rows // n_grp
    loop_pos = lax.axis_index("loop")
    grp_pos = lax.axis_index("grp")
    core = lax.rem(loop_pos, 2)

    def on_loop(by):
        return (lax.rem(loop_pos + by + n_loop, n_loop), grp_pos)

    bits = [lax.rem(grp_pos // (1 << i), 2) for i in range(n_grp.bit_length() - 1)]

    def grp_peer(b):
        peer = grp_pos
        for i, bit in enumerate(bits):
            if (b >> i) & 1:
                peer = peer + (1 - 2 * bit) * (1 << i)
        return (loop_pos, peer)

    sibling = on_loop(1 - 2 * core)
    ahead, behind = on_loop(2), on_loop(-2)
    far = on_loop(6 * core - 3)

    barrier = pltpu.get_barrier_semaphore()
    peers = [grp_peer(b) for b in BUCKET_ORDER] + [sibling, ahead, behind, far]
    for peer in peers:
        pl.semaphore_signal(barrier, inc=1, device_id=peer, device_id_type=MESH)

    loads = [
        pltpu.make_async_copy(k_hbm, tiles.at[0, 0], local_sem.at[0]),
        pltpu.make_async_copy(v_hbm, tiles.at[0, 1], local_sem.at[1]),
        pltpu.make_async_copy(order_hbm, order_ref, local_sem.at[2]),
        pltpu.make_async_copy(q_hbm, q_vmem, local_sem.at[3]),
        pltpu.make_async_copy(tile_hbm, tile_ref, local_sem.at[4]),
        pltpu.make_async_copy(bias_hbm, bias_ref, local_sem.at[5]),
    ]
    for load in loads:
        load.start()

    row_id = lax.broadcasted_iota(jnp.int32, (rows, rows), 0)

    def gather(j):
        hot = (row_id == order_ref[j : j + 1, :]).astype(jnp.float32)
        pick = jnp.transpose(hot).astype(jnp.bfloat16)
        for part in range(2):
            send_buf[j, :, part * width : (part + 1) * width] = jnp.dot(
                pick, tiles[0, part], preferred_element_type=jnp.float32
            ).astype(jnp.bfloat16)

    def exp_copy(j, b):
        where = pl.ds(b * bucket, bucket)
        return pltpu.make_async_remote_copy(
            src_ref=send_buf.at[j, where],
            dst_ref=recv_buf.at[j, where],
            send_sem=exp_send.at[j, b],
            recv_sem=exp_recv.at[j, b],
            device_id=grp_peer(b),
            device_id_type=MESH,
        )

    def tile_copy(src, slot, to):
        return pltpu.make_async_remote_copy(
            src_ref=tiles.at[src],
            dst_ref=tiles.at[slot],
            send_sem=tile_send.at[slot],
            recv_sem=tile_recv.at[slot],
            device_id=to,
            device_id_type=MESH,
        )

    to_far = tile_copy(0, 6, far)
    to_ahead = tile_copy(0, 2, ahead)
    to_behind = tile_copy(0, 3, behind)
    to_sibling = tile_copy(0, 1, sibling)
    pass_behind = tile_copy(2, 4, sibling)
    pass_ahead = tile_copy(3, 5, sibling)

    for load in loads[:3]:
        load.wait()
    gather(0)
    pl.semaphore_wait(barrier, len(peers))
    for copy in (to_ahead, to_behind, to_far, to_sibling):
        copy.start()
    for b in BUCKET_ORDER:
        exp_copy(0, b).start()
    for j in range(1, matchings):
        gather(j)
        for b in BUCKET_ORDER:
            exp_copy(j, b).start()

    for load in loads[3:]:
        load.wait()
    scale = head**-0.5
    q_scaled = q_vmem[...].astype(jnp.float32) * scale
    q_turned = jnp.transpose(q_scaled).astype(jnp.bfloat16)
    q_blocks[...] = jnp.zeros_like(q_blocks)
    for h in range(heads):
        i, half = h // 2, h % 2
        q_blocks[i, half * head : (half + 1) * head, half * rows : (half + 1) * rows] = (
            q_turned[h * head : (h + 1) * head, :]
        )
    run_max[...] = jnp.full_like(run_max, NEG_FILL)
    run_sum[...] = jnp.zeros_like(run_sum)
    run_acc[...] = jnp.zeros_like(run_acc)

    def absorb(slot, offset):
        wanted = tile_ref[0, 0] == offset + RADIUS
        for t in range(1, tile_ref.shape[1]):
            wanted = jnp.logical_or(wanted, tile_ref[0, t] == offset + RADIUS)
        fill = jnp.where(wanted, 0.0, NEG_FILL)
        v_turned = jnp.transpose(tiles[slot, 1].astype(jnp.float32)).astype(jnp.bfloat16)
        for i in range(heads // 2):
            pair = jnp.dot(
                tiles[slot, 0, :, i * 2 * head : (i + 1) * 2 * head],
                q_blocks[i],
                preferred_element_type=jnp.float32,
            )
            for half in range(2):
                h = 2 * i + half
                scores = pair[:, half * rows : (half + 1) * rows]
                old = run_max[h : h + 1, :]
                new = jnp.maximum(old, jnp.max(scores, axis=0, keepdims=True) + fill)
                weights = jnp.exp(scores - (new - fill))
                rescale = jnp.exp(old - new)
                run_max[h : h + 1, :] = new
                run_sum[h : h + 1, :] = run_sum[h : h + 1, :] * rescale + jnp.sum(
                    weights, axis=0, keepdims=True
                )
                here = slice(h * head, (h + 1) * head)
                run_acc[here, :] = run_acc[here, :] * rescale + jnp.dot(
                    v_turned[here, :],
                    weights.astype(jnp.bfloat16),
                    preferred_element_type=jnp.float32,
                )

    @pl.loop(0, 7)
    def _(slot):
        @pl.when(slot > 0)
        def _():
            tile_copy(0, slot, sibling).wait_recv()

        @pl.when(slot == 2)
        def _():
            pass_behind.start()

        @pl.when(slot == 3)
        def _():
            pass_ahead.start()

        near = 1 - 2 * core
        offset = jnp.where(
            slot < 2,
            slot * near,
            jnp.where(
                slot == 2,
                -2,
                jnp.where(
                    slot == 3,
                    2,
                    jnp.where(
                        slot == 4,
                        -1 - 2 * core,
                        jnp.where(slot == 5, 3 - 2 * core, 6 * core - 3),
                    ),
                ),
            ),
        )
        absorb(slot, offset)

    acc_rows[...] = jnp.transpose(run_acc[...])

    head_id = lax.broadcasted_iota(jnp.int32, (heads, width), 0)
    lane_id = lax.broadcasted_iota(jnp.int32, (heads, width), 1)
    in_head = jnp.logical_and(lane_id >= head_id * head, lane_id < (head_id + 1) * head)
    in_head = in_head.astype(jnp.float32).astype(jnp.bfloat16)
    bias_row = lax.broadcasted_iota(jnp.int32, (heads, rows), 0)
    lane = lax.broadcasted_iota(jnp.int32, (8, rows), 1)

    def split(x):
        high = x.astype(jnp.bfloat16)
        return high, (x - high.astype(jnp.float32)).astype(jnp.bfloat16)

    def expander(j):
        for b in BUCKET_ORDER:
            exp_copy(j, b).wait_recv()
        recv_buf[j, 0:bucket, :] = send_buf[j, 0:bucket, :]
        order = jnp.broadcast_to(order_ref[j : j + 1, :], (8, rows))
        swapped = jnp.where(
            lax.rem(lane, 2) == 0, pltpu.roll(order, rows - 1, 1), pltpu.roll(order, 1, 1)
        )
        order = jnp.where(lane < bucket, swapped, order)[0:1, :]
        back = (row_id == order).astype(jnp.float32).astype(jnp.bfloat16)
        keys = jnp.dot(back, recv_buf[j, :, :width], preferred_element_type=jnp.float32)
        partner_vals[j] = jnp.dot(
            back, recv_buf[j, :, width:], preferred_element_type=jnp.float32
        )
        terms = keys * (q_vmem[...].astype(jnp.float32) * scale)
        score = jnp.zeros((heads, rows), jnp.float32)
        for term in split(terms):
            score = score + lax.dot_general(
                in_head, term, (((1,), (1,)), ((), ())), preferred_element_type=jnp.float32
            )
        for h in range(heads):
            score = score + jnp.where(bias_row == h, bias_ref[j, h], 0.0)
        expander_e[j] = score

    for j in range(matchings):
        expander(j)

    top = run_max[...]
    for j in range(matchings):
        top = jnp.maximum(top, expander_e[j])
    block_part = jnp.exp(run_max[...] - top)
    weights = [jnp.exp(expander_e[j] - top) for j in range(matchings)]
    total = run_sum[...] * block_part
    for weight in weights:
        total = total + weight

    def spread(x):
        both = jnp.concatenate(split(x), axis=0)
        twice = jnp.concatenate([in_head, in_head], axis=0)
        return lax.dot_general(
            both, twice, (((0,), (0,)), ((), ())), preferred_element_type=jnp.float32
        )

    inverse = 1.0 / total
    attended = spread(block_part * inverse) * acc_rows[...]
    for j, weight in enumerate(weights):
        weight = weight.astype(jnp.bfloat16).astype(jnp.float32)
        attended = attended + spread(weight * inverse) * partner_vals[j]
    att_ref[...] = attended.astype(jnp.bfloat16)

    for copy in (to_ahead, to_behind, to_far, to_sibling, pass_behind, pass_ahead):
        copy.wait_send()
    for j in range(matchings):
        for b in BUCKET_ORDER:
            exp_copy(j, b).wait_send()


def solution(mesh):
    n_loop, n_grp = mesh.shape["loop"], mesh.shape["grp"]

    def shards(queries, key_rows, value_rows, out_weight, tile_list, order, bias):
        rows, width = queries.shape
        matchings, heads = bias.shape
        head = width // heads
        hbm = pl.BlockSpec(memory_space=pltpu.MemorySpace.HBM)
        vmem = pl.BlockSpec(memory_space=pltpu.VMEM)

        def body(*refs):
            kernel((n_loop, n_grp, matchings, heads, head), *refs)

        attended = pl.pallas_call(
            body,
            out_shape=jax.ShapeDtypeStruct((rows, width), jnp.bfloat16),
            in_specs=[hbm] * 6,
            out_specs=vmem,
            scratch_shapes=[
                pltpu.VMEM(order.shape, order.dtype),
                pltpu.SMEM(tile_list.shape, tile_list.dtype),
                pltpu.SMEM(bias.shape, bias.dtype),
                pltpu.VMEM((7, 2, rows, width), jnp.bfloat16),
                pltpu.VMEM((rows, width), jnp.bfloat16),
                pltpu.VMEM((heads // 2, 2 * head, 2 * rows), jnp.bfloat16),
                pltpu.VMEM((matchings, rows, 2 * width), jnp.bfloat16),
                pltpu.VMEM((matchings, rows, 2 * width), jnp.bfloat16),
                pltpu.VMEM((heads, rows), jnp.float32),
                pltpu.VMEM((heads, rows), jnp.float32),
                pltpu.VMEM((width, rows), jnp.float32),
                pltpu.VMEM((rows, width), jnp.float32),
                pltpu.VMEM((matchings, rows, width), jnp.float32),
                pltpu.VMEM((matchings, heads, rows), jnp.float32),
                pltpu.SemaphoreType.DMA((6,)),
                pltpu.SemaphoreType.DMA((7,)),
                pltpu.SemaphoreType.DMA((7,)),
                pltpu.SemaphoreType.DMA((matchings, n_grp)),
                pltpu.SemaphoreType.DMA((matchings, n_grp)),
            ],
            compiler_params=pltpu.CompilerParams(
                collective_id=0, has_side_effects=True, vmem_limit_bytes=62 * 2**20
            ),
        )(queries, key_rows, value_rows, order, tile_list, bias)
        return jnp.dot(attended, out_weight, preferred_element_type=jnp.float32).astype(
            jnp.bfloat16
        )

    rows_spec = P(("loop", "grp"), None)
    return jax.shard_map(
        shards,
        mesh=mesh,
        in_specs=(rows_spec, rows_spec, rows_spec, P(), rows_spec, P(None, ("loop", "grp")), P()),
        out_specs=rows_spec,
        check_vma=False,
    )
```

```python
import jax
import jax.numpy as jnp
from jax import lax
from jax.experimental import pallas as pl
from jax.experimental.pallas import tpu as pltpu
from jax.sharding import PartitionSpec as P

MESH = pl.DeviceIdType.MESH
NEG_FILL = -1e30
RADIUS = 3
X_RING = 4
BUCKET_ORDER = (15, 1, 8, 2, 14, 3, 9, 4, 13, 5, 10, 6, 12, 7, 11)


def kernel(
    sizes,
    q_hbm,
    k_hbm,
    v_hbm,
    order_hbm,
    tile_hbm,
    bias_hbm,
    att_ref,
    order_ref,
    tile_ref,
    bias_ref,
    tiles,
    q_vmem,
    q_blocks,
    send_buf,
    recv_buf,
    run_max,
    run_sum,
    run_acc,
    acc_rows,
    partner_vals,
    expander_e,
    local_sem,
    tile_send,
    tile_recv,
    exp_send,
    exp_recv,
):
    n_loop, n_grp, matchings, heads, head = sizes
    rows, width = q_vmem.shape
    bucket = rows // n_grp
    loop_pos = lax.axis_index("loop")
    grp_pos = lax.axis_index("grp")
    core = lax.rem(loop_pos, 2)

    def on_loop(by):
        return (lax.rem(loop_pos + by + n_loop, n_loop), grp_pos)

    bits = [lax.rem(grp_pos // (1 << i), 2) for i in range(n_grp.bit_length() - 1)]

    def grp_peer(b):
        peer = grp_pos
        for i, bit in enumerate(bits):
            if (b >> i) & 1:
                peer = peer + (1 - 2 * bit) * (1 << i)
        return (loop_pos, peer)

    sibling = on_loop(1 - 2 * core)
    ahead, behind = on_loop(2), on_loop(-2)
    far = on_loop(6 * core - 3)
    beyond = on_loop(10 * core - 5)
    across = on_loop(8 * core - 4)
    place = lax.rem(loop_pos // 2, X_RING)
    first_core, last_core = core == 0, core == 1
    at_first, at_last = place == 0, place == X_RING - 1
    at_end = jnp.logical_or(
        jnp.logical_and(at_first, first_core), jnp.logical_and(at_last, last_core)
    )
    past_end = jnp.logical_or(
        jnp.logical_and(at_first, last_core), jnp.logical_and(at_last, first_core)
    )
    before_end = jnp.logical_or(
        jnp.logical_and(place == 1, first_core), jnp.logical_and(place == X_RING - 2, last_core)
    )

    barrier = pltpu.get_barrier_semaphore()
    peers = [grp_peer(b) for b in BUCKET_ORDER] + [
        sibling,
        ahead,
        behind,
        far,
        beyond,
        on_loop(4),
        on_loop(-4),
    ]
    for peer in peers:
        pl.semaphore_signal(barrier, inc=1, device_id=peer, device_id_type=MESH)

    loads = [
        pltpu.make_async_copy(k_hbm, tiles.at[0, 0], local_sem.at[0]),
        pltpu.make_async_copy(v_hbm, tiles.at[0, 1], local_sem.at[1]),
        pltpu.make_async_copy(order_hbm, order_ref, local_sem.at[2]),
        pltpu.make_async_copy(q_hbm, q_vmem, local_sem.at[3]),
        pltpu.make_async_copy(tile_hbm, tile_ref, local_sem.at[4]),
        pltpu.make_async_copy(bias_hbm, bias_ref, local_sem.at[5]),
    ]
    for load in loads:
        load.start()

    row_id = lax.broadcasted_iota(jnp.int32, (rows, rows), 0)

    def gather(j):
        hot = (row_id == order_ref[j : j + 1, :]).astype(jnp.float32)
        pick = jnp.transpose(hot).astype(jnp.bfloat16)
        for part in range(2):
            send_buf[j, :, part * width : (part + 1) * width] = jnp.dot(
                pick, tiles[0, part], preferred_element_type=jnp.float32
            ).astype(jnp.bfloat16)

    def exp_copy(j, b):
        where = pl.ds(b * bucket, bucket)
        return pltpu.make_async_remote_copy(
            src_ref=send_buf.at[j, where],
            dst_ref=recv_buf.at[j, where],
            send_sem=exp_send.at[j, b],
            recv_sem=exp_recv.at[j, b],
            device_id=grp_peer(b),
            device_id_type=MESH,
        )

    def tile_copy(src, slot, to, send, part):
        return pltpu.make_async_remote_copy(
            src_ref=tiles.at[src, part],
            dst_ref=tiles.at[slot, part],
            send_sem=tile_send.at[send, part],
            recv_sem=tile_recv.at[slot, part],
            device_id=to,
            device_id_type=MESH,
        )

    def both(*args):
        return [tile_copy(*args, part) for part in range(2)]

    to_sibling = both(0, 1, sibling, 1)
    to_ahead = both(0, 2, ahead, 2)
    to_behind = both(0, 3, behind, 3)
    pass_near = [None, None, both(2, 4, sibling, 4), both(3, 5, sibling, 5)]
    to_far = both(0, 6, far, 6)
    pass_round = [
        None,
        None,
        [tile_copy(2, 3, across, 7, 1), tile_copy(2, 6, beyond, 0, 1)],
        [tile_copy(3, 2, across, 7, 1), tile_copy(3, 6, beyond, 0, 1)],
    ]
    keep_ahead = jnp.logical_and(at_last, last_core)
    keep_behind = jnp.logical_and(at_first, first_core)

    def unless(flag, copies, act):
        @pl.when(jnp.logical_not(flag))
        def _():
            for copy in copies:
                act(copy)

    def own_tiles(act):
        unless(keep_ahead, to_ahead[1:], act)
        unless(keep_behind, to_behind[1:], act)
        act(to_ahead[0])
        act(to_behind[0])
        for copy in to_sibling[::-1]:
            act(copy)
        unless(at_end, to_far[1:], act)
        act(to_far[0])

    def passed_on(near, part, act):
        if part == 1:
            carries = first_core if near == 2 else last_core
            unless(jnp.logical_not(jnp.logical_and(before_end, carries)), pass_round[near], act)
        act(pass_near[near][part])

    def begin(copy):
        copy.start()

    def sent(copy):
        copy.wait_send()

    for load in loads[:3]:
        load.wait()
    gather(0)
    pl.semaphore_wait(barrier, len(peers))
    early_half = grp_pos < n_grp // 2

    @pl.when(early_half)
    def _():
        own_tiles(begin)
        for b in BUCKET_ORDER:
            exp_copy(0, b).start()
        gather(1)
        for b in BUCKET_ORDER:
            exp_copy(1, b).start()
        gather(2)
        for b in BUCKET_ORDER:
            exp_copy(2, b).start()

    @pl.when(jnp.logical_not(early_half))
    def _():
        for b in BUCKET_ORDER:
            exp_copy(0, b).start()
        gather(1)
        own_tiles(begin)
        for b in BUCKET_ORDER:
            exp_copy(1, b).start()
        gather(2)
        for b in BUCKET_ORDER:
            exp_copy(2, b).start()


    for load in loads[3:]:
        load.wait()
    scale = head**-0.5
    q_scaled = q_vmem[...].astype(jnp.float32) * scale
    q_turned = jnp.transpose(q_scaled).astype(jnp.bfloat16)
    q_blocks[...] = jnp.zeros_like(q_blocks)
    for h in range(heads):
        i, half = h // 2, h % 2
        q_blocks[i, half * head : (half + 1) * head, half * rows : (half + 1) * rows] = (
            q_turned[h * head : (h + 1) * head, :]
        )
    run_max[...] = jnp.full_like(run_max, NEG_FILL)
    run_sum[...] = jnp.zeros_like(run_sum)
    run_acc[...] = jnp.zeros_like(run_acc)

    def absorb(slot, offset):
        wanted = tile_ref[0, 0] == offset + RADIUS
        for t in range(1, tile_ref.shape[1]):
            wanted = jnp.logical_or(wanted, tile_ref[0, t] == offset + RADIUS)
        fill = jnp.where(wanted, 0.0, NEG_FILL)
        v_turned = jnp.transpose(tiles[slot, 1].astype(jnp.float32)).astype(jnp.bfloat16)
        for i in range(heads // 2):
            pair = jnp.dot(
                tiles[slot, 0, :, i * 2 * head : (i + 1) * 2 * head],
                q_blocks[i],
                preferred_element_type=jnp.float32,
            )
            for half in range(2):
                h = 2 * i + half
                scores = pair[:, half * rows : (half + 1) * rows]
                old = run_max[h : h + 1, :]
                new = jnp.maximum(old, jnp.max(scores, axis=0, keepdims=True) + fill)
                weights = jnp.exp(scores - (new - fill))
                rescale = jnp.exp(old - new)
                run_max[h : h + 1, :] = new
                run_sum[h : h + 1, :] = run_sum[h : h + 1, :] * rescale + jnp.sum(
                    weights, axis=0, keepdims=True
                )
                here = slice(h * head, (h + 1) * head)
                run_acc[here, :] = run_acc[here, :] * rescale + jnp.dot(
                    v_turned[here, :],
                    weights.astype(jnp.bfloat16),
                    preferred_element_type=jnp.float32,
                )

    head_id = lax.broadcasted_iota(jnp.int32, (heads, width), 0)
    lane_id = lax.broadcasted_iota(jnp.int32, (heads, width), 1)
    in_head = jnp.logical_and(lane_id >= head_id * head, lane_id < (head_id + 1) * head)
    in_head = in_head.astype(jnp.float32).astype(jnp.bfloat16)
    bias_row = lax.broadcasted_iota(jnp.int32, (heads, rows), 0)
    lane = lax.broadcasted_iota(jnp.int32, (8, rows), 1)

    def split(x):
        high = x.astype(jnp.bfloat16)
        return high, (x - high.astype(jnp.float32)).astype(jnp.bfloat16)

    def expander(j):
        for b in BUCKET_ORDER:
            exp_copy(j, b).wait_recv()
        recv_buf[j, 0:bucket, :] = send_buf[j, 0:bucket, :]
        order = jnp.broadcast_to(order_ref[j : j + 1, :], (8, rows))
        swapped = jnp.where(
            lax.rem(lane, 2) == 0, pltpu.roll(order, rows - 1, 1), pltpu.roll(order, 1, 1)
        )
        order = jnp.where(lane < bucket, swapped, order)[0:1, :]
        back = (row_id == order).astype(jnp.float32).astype(jnp.bfloat16)
        keys = jnp.dot(back, recv_buf[j, :, :width], preferred_element_type=jnp.float32)
        partner_vals[j] = jnp.dot(
            back, recv_buf[j, :, width:], preferred_element_type=jnp.float32
        )
        terms = keys * (q_vmem[...].astype(jnp.float32) * scale)
        score = jnp.zeros((heads, rows), jnp.float32)
        for term in split(terms):
            score = score + lax.dot_general(
                in_head, term, (((1,), (1,)), ((), ())), preferred_element_type=jnp.float32
            )
        for h in range(heads):
            score = score + jnp.where(bias_row == h, bias_ref[j, h], 0.0)
        expander_e[j] = score

    early = jnp.where(lax.rem(place, 2) == 0, 3, 2)

    at_edge = jnp.logical_or(at_first, at_last)
    far_soon = past_end
    expander_step = (4, jnp.where(at_edge, 4, 6), jnp.where(at_edge, 5, 7))

    @pl.loop(0, 8)
    def _(step):
        for j in range(matchings):

            @pl.when(step == expander_step[j])
            def _():
                expander(j)

        @pl.when(step < 7)
        def _():
            late = jnp.where(far_soon, jnp.where(step == 4, 6, step - 1), step)
            late = jnp.where(jnp.logical_and(far_soon, step < 4), step, late)
            slot = jnp.where(
                step < 2,
                step,
                jnp.where(
                    step == 2,
                    early,
                    jnp.where(
                        step == 3,
                        early + 2,
                        jnp.where(late == 4, 5 - early, jnp.where(late == 5, 7 - early, 6)),
                    ),
                ),
            )

            for part in (1, 0):

                @pl.when(step > 0)
                def _():
                    tile_copy(0, slot, sibling, 1, part).wait_recv()

                for near in (2, 3):

                    @pl.when(slot == near)
                    def _():
                        passed_on(near, part, begin)

            offset = jnp.where(
                slot < 2,
                slot * (1 - 2 * core),
                jnp.where(
                    slot == 2,
                    -2,
                    jnp.where(
                        slot == 3,
                        2,
                        jnp.where(
                            slot == 4,
                            -1 - 2 * core,
                            jnp.where(slot == 5, 3 - 2 * core, 6 * core - 3),
                        ),
                    ),
                ),
            )
            absorb(slot, offset)

    acc_rows[...] = jnp.transpose(run_acc[...])


    top = run_max[...]
    for j in range(matchings):
        top = jnp.maximum(top, expander_e[j])
    block_part = jnp.exp(run_max[...] - top)
    weights = [jnp.exp(expander_e[j] - top) for j in range(matchings)]
    total = run_sum[...] * block_part
    for weight in weights:
        total = total + weight

    def spread(x):
        both = jnp.concatenate(split(x), axis=0)
        twice = jnp.concatenate([in_head, in_head], axis=0)
        return lax.dot_general(
            both, twice, (((0,), (0,)), ((), ())), preferred_element_type=jnp.float32
        )

    inverse = 1.0 / total
    attended = spread(block_part * inverse) * acc_rows[...]
    for j, weight in enumerate(weights):
        weight = weight.astype(jnp.bfloat16).astype(jnp.float32)
        attended = attended + spread(weight * inverse) * partner_vals[j]
    att_ref[...] = attended.astype(jnp.bfloat16)

    own_tiles(sent)
    for near in (2, 3):
        for part in range(2):
            passed_on(near, part, sent)
    for j in range(matchings):
        for b in BUCKET_ORDER:
            exp_copy(j, b).wait_send()


def solution(mesh):
    n_loop, n_grp = mesh.shape["loop"], mesh.shape["grp"]

    def shards(queries, key_rows, value_rows, out_weight, tile_list, order, bias):
        rows, width = queries.shape
        matchings, heads = bias.shape
        head = width // heads
        hbm = pl.BlockSpec(memory_space=pltpu.MemorySpace.HBM)
        vmem = pl.BlockSpec(memory_space=pltpu.VMEM)

        def body(*refs):
            kernel((n_loop, n_grp, matchings, heads, head), *refs)

        attended = pl.pallas_call(
            body,
            out_shape=jax.ShapeDtypeStruct((rows, width), jnp.bfloat16),
            in_specs=[hbm] * 6,
            out_specs=vmem,
            scratch_shapes=[
                pltpu.VMEM(order.shape, order.dtype),
                pltpu.SMEM(tile_list.shape, tile_list.dtype),
                pltpu.SMEM(bias.shape, bias.dtype),
                pltpu.VMEM((7, 2, rows, width), jnp.bfloat16),
                pltpu.VMEM((rows, width), jnp.bfloat16),
                pltpu.VMEM((heads // 2, 2 * head, 2 * rows), jnp.bfloat16),
                pltpu.VMEM((matchings, rows, 2 * width), jnp.bfloat16),
                pltpu.VMEM((matchings, rows, 2 * width), jnp.bfloat16),
                pltpu.VMEM((heads, rows), jnp.float32),
                pltpu.VMEM((heads, rows), jnp.float32),
                pltpu.VMEM((width, rows), jnp.float32),
                pltpu.VMEM((rows, width), jnp.float32),
                pltpu.VMEM((matchings, rows, width), jnp.float32),
                pltpu.VMEM((matchings, heads, rows), jnp.float32),
                pltpu.SemaphoreType.DMA((6,)),
                pltpu.SemaphoreType.DMA((8, 2)),
                pltpu.SemaphoreType.DMA((7, 2)),
                pltpu.SemaphoreType.DMA((matchings, n_grp)),
                pltpu.SemaphoreType.DMA((matchings, n_grp)),
            ],
            compiler_params=pltpu.CompilerParams(
                collective_id=0, has_side_effects=True, vmem_limit_bytes=40 * 2**20
            ),
        )(
            *(
                pltpu.with_memory_space_constraint(x, pltpu.MemorySpace.HBM)
                for x in (queries, key_rows, value_rows, order, tile_list, bias)
            )
        )
        return jnp.dot(attended, out_weight, preferred_element_type=jnp.float32).astype(
            jnp.bfloat16
        )

    rows_spec = P(("loop", "grp"), None)
    return jax.shard_map(
        shards,
        mesh=mesh,
        in_specs=(rows_spec, rows_spec, rows_spec, P(), rows_spec, P(None, ("loop", "grp")), P()),
        out_specs=rows_spec,
        check_vma=False,
    )
```

```python
import jax
import jax.numpy as jnp
from jax import lax
from jax.experimental import pallas as pl
from jax.experimental.pallas import tpu as pltpu
from jax.sharding import PartitionSpec as P

MESH = pl.DeviceIdType.MESH
NEG_FILL = -1e30
RADIUS = 3
X_RING = 4
BUCKET_ORDER = (15, 1, 8, 2, 14, 3, 9, 4, 13, 5, 10, 6, 12, 7, 11)


def kernel(
    sizes,
    q_hbm,
    k_hbm,
    v_hbm,
    order_hbm,
    tile_hbm,
    bias_hbm,
    att_ref,
    order_ref,
    tile_ref,
    bias_ref,
    tiles,
    q_vmem,
    q_blocks,
    send_buf,
    recv_buf,
    run_max,
    run_sum,
    run_acc,
    acc_rows,
    partner_vals,
    expander_e,
    local_sem,
    tile_send,
    tile_recv,
    exp_send,
    exp_recv,
):
    n_loop, n_grp, matchings, heads, head = sizes
    rows, width = q_vmem.shape
    bucket = rows // n_grp
    loop_pos = lax.axis_index("loop")
    grp_pos = lax.axis_index("grp")
    core = lax.rem(loop_pos, 2)

    def on_loop(by):
        return (lax.rem(loop_pos + by + n_loop, n_loop), grp_pos)

    bits = [lax.rem(grp_pos // (1 << i), 2) for i in range(n_grp.bit_length() - 1)]

    def grp_peer(b):
        peer = grp_pos
        for i, bit in enumerate(bits):
            if (b >> i) & 1:
                peer = peer + (1 - 2 * bit) * (1 << i)
        return (loop_pos, peer)

    sibling = on_loop(1 - 2 * core)
    ahead, behind = on_loop(2), on_loop(-2)
    far = on_loop(6 * core - 3)
    beyond = on_loop(10 * core - 5)
    across = on_loop(8 * core - 4)
    place = lax.rem(loop_pos // 2, X_RING)
    first_core, last_core = core == 0, core == 1
    at_first, at_last = place == 0, place == X_RING - 1
    at_end = jnp.logical_or(
        jnp.logical_and(at_first, first_core), jnp.logical_and(at_last, last_core)
    )
    past_end = jnp.logical_or(
        jnp.logical_and(at_first, last_core), jnp.logical_and(at_last, first_core)
    )
    before_end = jnp.logical_or(
        jnp.logical_and(place == 1, first_core), jnp.logical_and(place == X_RING - 2, last_core)
    )

    barrier = pltpu.get_barrier_semaphore()
    peers = [grp_peer(b) for b in BUCKET_ORDER] + [
        sibling,
        ahead,
        behind,
        far,
        beyond,
        on_loop(4),
        on_loop(-4),
    ]
    for peer in peers:
        pl.semaphore_signal(barrier, inc=1, device_id=peer, device_id_type=MESH)

    loads = [
        pltpu.make_async_copy(k_hbm, tiles.at[0, 0], local_sem.at[0]),
        pltpu.make_async_copy(v_hbm, tiles.at[0, 1], local_sem.at[1]),
        pltpu.make_async_copy(order_hbm, order_ref, local_sem.at[2]),
        pltpu.make_async_copy(q_hbm, q_vmem, local_sem.at[3]),
        pltpu.make_async_copy(tile_hbm, tile_ref, local_sem.at[4]),
        pltpu.make_async_copy(bias_hbm, bias_ref, local_sem.at[5]),
    ]
    for load in loads:
        load.start()

    row_id = lax.broadcasted_iota(jnp.int32, (rows, rows), 0)

    def gather(j):
        hot = (row_id == order_ref[j : j + 1, :]).astype(jnp.float32)
        pick = jnp.transpose(hot).astype(jnp.bfloat16)
        for part in range(2):
            send_buf[j, :, part * width : (part + 1) * width] = jnp.dot(
                pick, tiles[0, part], preferred_element_type=jnp.float32
            ).astype(jnp.bfloat16)

    def exp_copy(j, b):
        where = pl.ds(b * bucket, bucket)
        return pltpu.make_async_remote_copy(
            src_ref=send_buf.at[j, where],
            dst_ref=recv_buf.at[j, where],
            send_sem=exp_send.at[j, b],
            recv_sem=exp_recv.at[j, b],
            device_id=grp_peer(b),
            device_id_type=MESH,
        )

    def tile_copy(src, slot, to, send, part):
        return pltpu.make_async_remote_copy(
            src_ref=tiles.at[src, part],
            dst_ref=tiles.at[slot, part],
            send_sem=tile_send.at[send, part],
            recv_sem=tile_recv.at[slot, part],
            device_id=to,
            device_id_type=MESH,
        )

    def both(*args):
        return [tile_copy(*args, part) for part in range(2)]

    to_sibling = both(0, 1, sibling, 1)
    to_ahead = both(0, 2, ahead, 2)
    to_behind = both(0, 3, behind, 3)
    pass_near = [None, None, both(2, 4, sibling, 4), both(3, 5, sibling, 5)]
    to_far = both(0, 6, far, 6)
    pass_round = [
        None,
        None,
        [tile_copy(2, 3, across, 7, 1), tile_copy(2, 6, beyond, 0, 1)],
        [tile_copy(3, 2, across, 7, 1), tile_copy(3, 6, beyond, 0, 1)],
    ]
    keep_ahead = jnp.logical_and(at_last, last_core)
    keep_behind = jnp.logical_and(at_first, first_core)

    def unless(flag, copies, act):
        @pl.when(jnp.logical_not(flag))
        def _():
            for copy in copies:
                act(copy)

    def own_tiles(act):
        unless(keep_ahead, to_ahead[1:], act)
        unless(keep_behind, to_behind[1:], act)
        act(to_ahead[0])
        act(to_behind[0])
        for copy in to_sibling[::-1]:
            act(copy)

    def far_tile(act):
        unless(at_end, to_far[1:], act)
        act(to_far[0])

    passes_end = jnp.logical_or(at_end, before_end)

    def passed_on(near, part, act):
        if part == 1:
            carries = first_core if near == 2 else last_core
            unless(jnp.logical_not(jnp.logical_and(before_end, carries)), pass_round[near], act)
        act(pass_near[near][part])

    def begin(copy):
        copy.start()

    def sent(copy):
        copy.wait_send()

    for load in loads[:3]:
        load.wait()
    gather(0)
    pl.semaphore_wait(barrier, len(peers))
    early_half = grp_pos < n_grp // 2

    @pl.when(early_half)
    def _():
        own_tiles(begin)
        pl.when(passes_end)(lambda: far_tile(begin))
        for b in BUCKET_ORDER:
            exp_copy(0, b).start()
        gather(1)
        for b in BUCKET_ORDER:
            exp_copy(1, b).start()
        gather(2)
        for b in BUCKET_ORDER:
            exp_copy(2, b).start()

    @pl.when(jnp.logical_not(early_half))
    def _():
        for b in BUCKET_ORDER:
            exp_copy(0, b).start()
        gather(1)
        own_tiles(begin)
        pl.when(passes_end)(lambda: far_tile(begin))
        for b in BUCKET_ORDER:
            exp_copy(1, b).start()
        gather(2)
        for b in BUCKET_ORDER:
            exp_copy(2, b).start()


    for load in loads[3:]:
        load.wait()
    scale = head**-0.5
    q_scaled = q_vmem[...].astype(jnp.float32) * scale
    q_turned = jnp.transpose(q_scaled).astype(jnp.bfloat16)
    q_blocks[...] = jnp.zeros_like(q_blocks)
    for h in range(heads):
        i, half = h // 2, h % 2
        q_blocks[i, half * head : (half + 1) * head, half * rows : (half + 1) * rows] = (
            q_turned[h * head : (h + 1) * head, :]
        )
    run_max[...] = jnp.full_like(run_max, NEG_FILL)
    run_sum[...] = jnp.zeros_like(run_sum)
    run_acc[...] = jnp.zeros_like(run_acc)

    def absorb(slot, offset):
        wanted = tile_ref[0, 0] == offset + RADIUS
        for t in range(1, tile_ref.shape[1]):
            wanted = jnp.logical_or(wanted, tile_ref[0, t] == offset + RADIUS)
        fill = jnp.where(wanted, 0.0, NEG_FILL)
        v_turned = jnp.transpose(tiles[slot, 1].astype(jnp.float32)).astype(jnp.bfloat16)
        old, total = run_max[...], run_sum[...]
        pairs = [
            jnp.dot(
                tiles[slot, 0, :, i * 2 * head : (i + 1) * 2 * head],
                q_blocks[i],
                preferred_element_type=jnp.float32,
            )
            for i in range(heads // 2)
        ]
        scores = [
            pairs[h // 2][:, (h % 2) * rows : (h % 2 + 1) * rows] for h in range(heads)
        ]
        tops = [jnp.max(score, axis=0, keepdims=True) for score in scores]
        new = jnp.maximum(old, jnp.concatenate(tops, axis=0) + fill)
        shift = new - fill
        rescale = jnp.exp(old - new)
        sums = []
        for h in range(heads):
            weights = jnp.exp(scores[h] - shift[h : h + 1, :])
            sums.append(jnp.sum(weights, axis=0, keepdims=True))
            here = slice(h * head, (h + 1) * head)
            run_acc[here, :] = run_acc[here, :] * rescale[h : h + 1, :] + jnp.dot(
                v_turned[here, :],
                weights.astype(jnp.bfloat16),
                preferred_element_type=jnp.float32,
            )
        run_max[...] = new
        run_sum[...] = total * rescale + jnp.concatenate(sums, axis=0)

    head_id = lax.broadcasted_iota(jnp.int32, (heads, width), 0)
    lane_id = lax.broadcasted_iota(jnp.int32, (heads, width), 1)
    in_head = jnp.logical_and(lane_id >= head_id * head, lane_id < (head_id + 1) * head)
    in_head = in_head.astype(jnp.float32).astype(jnp.bfloat16)
    bias_row = lax.broadcasted_iota(jnp.int32, (heads, rows), 0)
    lane = lax.broadcasted_iota(jnp.int32, (8, rows), 1)

    def split(x):
        high = x.astype(jnp.bfloat16)
        return high, (x - high.astype(jnp.float32)).astype(jnp.bfloat16)

    def expander(j):
        for b in BUCKET_ORDER:
            exp_copy(j, b).wait_recv()
        recv_buf[j, 0:bucket, :] = send_buf[j, 0:bucket, :]
        order = jnp.broadcast_to(order_ref[j : j + 1, :], (8, rows))
        swapped = jnp.where(
            lax.rem(lane, 2) == 0, pltpu.roll(order, rows - 1, 1), pltpu.roll(order, 1, 1)
        )
        order = jnp.where(lane < bucket, swapped, order)[0:1, :]
        back = (row_id == order).astype(jnp.float32).astype(jnp.bfloat16)
        keys = jnp.dot(back, recv_buf[j, :, :width], preferred_element_type=jnp.float32)
        partner_vals[j] = jnp.dot(
            back, recv_buf[j, :, width:], preferred_element_type=jnp.float32
        )
        terms = keys * (q_vmem[...].astype(jnp.float32) * scale)
        score = jnp.zeros((heads, rows), jnp.float32)
        for term in split(terms):
            score = score + lax.dot_general(
                in_head, term, (((1,), (1,)), ((), ())), preferred_element_type=jnp.float32
            )
        for h in range(heads):
            score = score + jnp.where(bias_row == h, bias_ref[j, h], 0.0)
        expander_e[j] = score

    early = jnp.where(lax.rem(place, 2) == 0, 3, 2)

    at_edge = jnp.logical_or(at_first, at_last)
    far_soon = at_edge
    expander_step = (4, jnp.where(at_edge, 4, 6), jnp.where(at_edge, 5, 7))

    @pl.loop(0, 8)
    def _(step):
        @pl.when(jnp.logical_and(step == 3, jnp.logical_not(passes_end)))
        def _():
            far_tile(begin)

        for j in range(matchings):

            @pl.when(step == expander_step[j])
            def _():
                expander(j)

        @pl.when(step < 7)
        def _():
            late = jnp.where(far_soon, jnp.where(step == 4, 6, step - 1), step)
            late = jnp.where(jnp.logical_and(far_soon, step < 4), step, late)
            slot = jnp.where(
                step < 2,
                step,
                jnp.where(
                    step == 2,
                    early,
                    jnp.where(
                        step == 3,
                        early + 2,
                        jnp.where(late == 4, 5 - early, jnp.where(late == 5, 7 - early, 6)),
                    ),
                ),
            )

            for part in (1, 0):

                @pl.when(step > 0)
                def _():
                    tile_copy(0, slot, sibling, 1, part).wait_recv()

                for near in (2, 3):

                    @pl.when(slot == near)
                    def _():
                        passed_on(near, part, begin)

            offset = jnp.where(
                slot < 2,
                slot * (1 - 2 * core),
                jnp.where(
                    slot == 2,
                    -2,
                    jnp.where(
                        slot == 3,
                        2,
                        jnp.where(
                            slot == 4,
                            -1 - 2 * core,
                            jnp.where(slot == 5, 3 - 2 * core, 6 * core - 3),
                        ),
                    ),
                ),
            )
            absorb(slot, offset)

    acc_rows[...] = jnp.transpose(run_acc[...])


    top = run_max[...]
    for j in range(matchings):
        top = jnp.maximum(top, expander_e[j])
    block_part = jnp.exp(run_max[...] - top)
    weights = [jnp.exp(expander_e[j] - top) for j in range(matchings)]
    total = run_sum[...] * block_part
    for weight in weights:
        total = total + weight

    def spread(x):
        both = jnp.concatenate(split(x), axis=0)
        twice = jnp.concatenate([in_head, in_head], axis=0)
        return lax.dot_general(
            both, twice, (((0,), (0,)), ((), ())), preferred_element_type=jnp.float32
        )

    inverse = 1.0 / total
    attended = spread(block_part * inverse) * acc_rows[...]
    for j, weight in enumerate(weights):
        weight = weight.astype(jnp.bfloat16).astype(jnp.float32)
        attended = attended + spread(weight * inverse) * partner_vals[j]
    att_ref[...] = attended.astype(jnp.bfloat16)

    own_tiles(sent)
    far_tile(sent)
    for near in (2, 3):
        for part in range(2):
            passed_on(near, part, sent)
    for j in range(matchings):
        for b in BUCKET_ORDER:
            exp_copy(j, b).wait_send()


def solution(mesh):
    n_loop, n_grp = mesh.shape["loop"], mesh.shape["grp"]

    def shards(queries, key_rows, value_rows, out_weight, tile_list, order, bias):
        rows, width = queries.shape
        matchings, heads = bias.shape
        head = width // heads
        hbm = pl.BlockSpec(memory_space=pltpu.MemorySpace.HBM)
        vmem = pl.BlockSpec(memory_space=pltpu.VMEM)

        def body(*refs):
            kernel((n_loop, n_grp, matchings, heads, head), *refs)

        attended = pl.pallas_call(
            body,
            out_shape=jax.ShapeDtypeStruct((rows, width), jnp.bfloat16),
            in_specs=[hbm] * 6,
            out_specs=vmem,
            scratch_shapes=[
                pltpu.VMEM(order.shape, order.dtype),
                pltpu.SMEM(tile_list.shape, tile_list.dtype),
                pltpu.SMEM(bias.shape, bias.dtype),
                pltpu.VMEM((7, 2, rows, width), jnp.bfloat16),
                pltpu.VMEM((rows, width), jnp.bfloat16),
                pltpu.VMEM((heads // 2, 2 * head, 2 * rows), jnp.bfloat16),
                pltpu.VMEM((matchings, rows, 2 * width), jnp.bfloat16),
                pltpu.VMEM((matchings, rows, 2 * width), jnp.bfloat16),
                pltpu.VMEM((heads, rows), jnp.float32),
                pltpu.VMEM((heads, rows), jnp.float32),
                pltpu.VMEM((width, rows), jnp.float32),
                pltpu.VMEM((rows, width), jnp.float32),
                pltpu.VMEM((matchings, rows, width), jnp.float32),
                pltpu.VMEM((matchings, heads, rows), jnp.float32),
                pltpu.SemaphoreType.DMA((6,)),
                pltpu.SemaphoreType.DMA((8, 2)),
                pltpu.SemaphoreType.DMA((7, 2)),
                pltpu.SemaphoreType.DMA((matchings, n_grp)),
                pltpu.SemaphoreType.DMA((matchings, n_grp)),
            ],
            compiler_params=pltpu.CompilerParams(
                collective_id=0, has_side_effects=True, vmem_limit_bytes=40 * 2**20
            ),
        )(
            *(
                pltpu.with_memory_space_constraint(x, pltpu.MemorySpace.HBM)
                for x in (queries, key_rows, value_rows, order, tile_list, bias)
            )
        )
        return jnp.dot(attended, out_weight, preferred_element_type=jnp.float32).astype(
            jnp.bfloat16
        )

    rows_spec = P(("loop", "grp"), None)
    return jax.shard_map(
        shards,
        mesh=mesh,
        in_specs=(rows_spec, rows_spec, rows_spec, P(), rows_spec, P(None, ("loop", "grp")), P()),
        out_specs=rows_spec,
        check_vma=False,
    )
```

```python
import jax
import jax.numpy as jnp
from jax import lax
from jax.experimental import pallas as pl
from jax.experimental.pallas import tpu as pltpu
from jax.sharding import PartitionSpec as P

MESH = pl.DeviceIdType.MESH
NEG_FILL = -1e30
RADIUS = 3
X_RING = 4
BUCKET_ORDER = (15, 1, 8, 2, 14, 3, 9, 4, 13, 5, 10, 6, 12, 7, 11)


def kernel(
    sizes,
    q_hbm,
    k_hbm,
    v_hbm,
    order_hbm,
    tile_hbm,
    bias_hbm,
    att_ref,
    order_ref,
    tile_ref,
    bias_ref,
    tiles,
    q_vmem,
    q_blocks,
    send_buf,
    recv_buf,
    run_max,
    run_sum,
    run_acc,
    acc_rows,
    partner_vals,
    expander_e,
    local_sem,
    tile_send,
    tile_recv,
    exp_send,
    exp_recv,
):
    n_loop, n_grp, matchings, heads, head = sizes
    rows, width = q_vmem.shape
    bucket = rows // n_grp
    loop_pos = lax.axis_index("loop")
    grp_pos = lax.axis_index("grp")
    core = lax.rem(loop_pos, 2)

    def on_loop(by):
        return (lax.rem(loop_pos + by + n_loop, n_loop), grp_pos)

    bits = [lax.rem(grp_pos // (1 << i), 2) for i in range(n_grp.bit_length() - 1)]

    def grp_peer(b):
        peer = grp_pos
        for i, bit in enumerate(bits):
            if (b >> i) & 1:
                peer = peer + (1 - 2 * bit) * (1 << i)
        return (loop_pos, peer)

    sibling = on_loop(1 - 2 * core)
    ahead, behind = on_loop(2), on_loop(-2)
    far = on_loop(6 * core - 3)
    beyond = on_loop(10 * core - 5)
    across = on_loop(8 * core - 4)
    place = lax.rem(loop_pos // 2, X_RING)
    first_core, last_core = core == 0, core == 1
    at_first, at_last = place == 0, place == X_RING - 1
    at_end = jnp.logical_or(
        jnp.logical_and(at_first, first_core), jnp.logical_and(at_last, last_core)
    )
    past_end = jnp.logical_or(
        jnp.logical_and(at_first, last_core), jnp.logical_and(at_last, first_core)
    )
    before_end = jnp.logical_or(
        jnp.logical_and(place == 1, first_core), jnp.logical_and(place == X_RING - 2, last_core)
    )

    barrier = pltpu.get_barrier_semaphore()
    peers = [grp_peer(b) for b in BUCKET_ORDER] + [
        sibling,
        ahead,
        behind,
        far,
        beyond,
        on_loop(4),
        on_loop(-4),
    ]
    for peer in peers:
        pl.semaphore_signal(barrier, inc=1, device_id=peer, device_id_type=MESH)

    loads = [
        pltpu.make_async_copy(k_hbm, tiles.at[0, 0], local_sem.at[0]),
        pltpu.make_async_copy(v_hbm, tiles.at[0, 1], local_sem.at[1]),
        pltpu.make_async_copy(order_hbm, order_ref, local_sem.at[2]),
        pltpu.make_async_copy(q_hbm, q_vmem, local_sem.at[3]),
        pltpu.make_async_copy(tile_hbm, tile_ref, local_sem.at[4]),
        pltpu.make_async_copy(bias_hbm, bias_ref, local_sem.at[5]),
    ]
    for load in loads:
        load.start()

    row_id = lax.broadcasted_iota(jnp.int32, (rows, rows), 0)

    def gather(j):
        hot = (row_id == order_ref[j : j + 1, :]).astype(jnp.float32)
        pick = jnp.transpose(hot).astype(jnp.bfloat16)
        for part in range(2):
            send_buf[j, :, part * width : (part + 1) * width] = jnp.dot(
                pick, tiles[0, part], preferred_element_type=jnp.float32
            ).astype(jnp.bfloat16)

    def exp_copy(j, b):
        where = pl.ds(b * bucket, bucket)
        return pltpu.make_async_remote_copy(
            src_ref=send_buf.at[j, where],
            dst_ref=recv_buf.at[j, where],
            send_sem=exp_send.at[j, b],
            recv_sem=exp_recv.at[j, b],
            device_id=grp_peer(b),
            device_id_type=MESH,
        )

    def tile_copy(src, slot, to, send, part):
        return pltpu.make_async_remote_copy(
            src_ref=tiles.at[src, part],
            dst_ref=tiles.at[slot, part],
            send_sem=tile_send.at[send, part],
            recv_sem=tile_recv.at[slot, part],
            device_id=to,
            device_id_type=MESH,
        )

    def both(*args):
        return [tile_copy(*args, part) for part in range(2)]

    to_sibling = both(0, 1, sibling, 1)
    to_ahead = both(0, 2, ahead, 2)
    to_behind = both(0, 3, behind, 3)
    pass_near = [None, None, both(2, 4, sibling, 4), both(3, 5, sibling, 5)]
    to_far = both(0, 6, far, 6)
    pass_round = [
        None,
        None,
        [tile_copy(2, 3, across, 7, 1), tile_copy(2, 6, beyond, 0, 1)],
        [tile_copy(3, 2, across, 7, 1), tile_copy(3, 6, beyond, 0, 1)],
    ]
    keep_ahead = jnp.logical_and(at_last, last_core)
    keep_behind = jnp.logical_and(at_first, first_core)

    def unless(flag, copies, act):
        @pl.when(jnp.logical_not(flag))
        def _():
            for copy in copies:
                act(copy)

    def own_tiles(act):
        unless(keep_ahead, to_ahead[1:], act)
        unless(keep_behind, to_behind[1:], act)
        act(to_ahead[0])
        act(to_behind[0])
        for copy in to_sibling[::-1]:
            act(copy)

    def far_tile(act):
        unless(at_end, to_far[1:], act)
        act(to_far[0])

    passes_end = jnp.logical_or(at_end, before_end)

    def passed_on(near, part, act):
        if part == 1:
            carries = first_core if near == 2 else last_core
            unless(jnp.logical_not(jnp.logical_and(before_end, carries)), pass_round[near], act)
        act(pass_near[near][part])

    def begin(copy):
        copy.start()

    def sent(copy):
        copy.wait_send()

    for load in loads[:3]:
        load.wait()
    gather(0)
    early_half = grp_pos < n_grp // 2

    @pl.when(early_half)
    def _():
        for j in range(1, matchings):
            gather(j)

    pl.semaphore_wait(barrier, len(peers))
    @pl.when(early_half)
    def _():
        own_tiles(begin)
        pl.when(passes_end)(lambda: far_tile(begin))
        for b in BUCKET_ORDER:
            exp_copy(0, b).start()
        for b in BUCKET_ORDER:
            exp_copy(1, b).start()
        for b in BUCKET_ORDER:
            exp_copy(2, b).start()

    @pl.when(jnp.logical_not(early_half))
    def _():
        for b in BUCKET_ORDER:
            exp_copy(0, b).start()
        gather(1)
        own_tiles(begin)
        pl.when(passes_end)(lambda: far_tile(begin))
        for b in BUCKET_ORDER:
            exp_copy(1, b).start()
        gather(2)
        for b in BUCKET_ORDER:
            exp_copy(2, b).start()


    for load in loads[3:]:
        load.wait()
    scale = head**-0.5
    q_scaled = q_vmem[...].astype(jnp.float32) * scale
    q_turned = jnp.transpose(q_scaled).astype(jnp.bfloat16)
    q_blocks[...] = jnp.zeros_like(q_blocks)
    for h in range(heads):
        i, half = h // 2, h % 2
        q_blocks[i, half * head : (half + 1) * head, half * rows : (half + 1) * rows] = (
            q_turned[h * head : (h + 1) * head, :]
        )
    run_max[...] = jnp.full_like(run_max, NEG_FILL)
    run_sum[...] = jnp.zeros_like(run_sum)
    run_acc[...] = jnp.zeros_like(run_acc)

    def absorb(slot, offset):
        wanted = tile_ref[0, 0] == offset + RADIUS
        for t in range(1, tile_ref.shape[1]):
            wanted = jnp.logical_or(wanted, tile_ref[0, t] == offset + RADIUS)
        fill = jnp.where(wanted, 0.0, NEG_FILL)
        v_turned = jnp.transpose(tiles[slot, 1].astype(jnp.float32)).astype(jnp.bfloat16)
        old, total = run_max[...], run_sum[...]
        pairs = [
            jnp.dot(
                tiles[slot, 0, :, i * 2 * head : (i + 1) * 2 * head],
                q_blocks[i],
                preferred_element_type=jnp.float32,
            )
            for i in range(heads // 2)
        ]
        scores = [
            pairs[h // 2][:, (h % 2) * rows : (h % 2 + 1) * rows] for h in range(heads)
        ]
        tops = [jnp.max(score, axis=0, keepdims=True) for score in scores]
        new = jnp.maximum(old, jnp.concatenate(tops, axis=0) + fill)
        shift = new - fill
        rescale = jnp.exp(old - new)
        sums = []
        for h in range(heads):
            weights = jnp.exp(scores[h] - shift[h : h + 1, :])
            sums.append(jnp.sum(weights, axis=0, keepdims=True))
            here = slice(h * head, (h + 1) * head)
            run_acc[here, :] = run_acc[here, :] * rescale[h : h + 1, :] + jnp.dot(
                v_turned[here, :],
                weights.astype(jnp.bfloat16),
                preferred_element_type=jnp.float32,
            )
        run_max[...] = new
        run_sum[...] = total * rescale + jnp.concatenate(sums, axis=0)

    head_id = lax.broadcasted_iota(jnp.int32, (heads, width), 0)
    lane_id = lax.broadcasted_iota(jnp.int32, (heads, width), 1)
    in_head = jnp.logical_and(lane_id >= head_id * head, lane_id < (head_id + 1) * head)
    in_head = in_head.astype(jnp.float32).astype(jnp.bfloat16)
    bias_row = lax.broadcasted_iota(jnp.int32, (heads, rows), 0)
    lane = lax.broadcasted_iota(jnp.int32, (8, rows), 1)

    def split(x):
        high = x.astype(jnp.bfloat16)
        return high, (x - high.astype(jnp.float32)).astype(jnp.bfloat16)

    def expander(j):
        for b in BUCKET_ORDER:
            exp_copy(j, b).wait_recv()
        recv_buf[j, 0:bucket, :] = send_buf[j, 0:bucket, :]
        order = jnp.broadcast_to(order_ref[j : j + 1, :], (8, rows))
        swapped = jnp.where(
            lax.rem(lane, 2) == 0, pltpu.roll(order, rows - 1, 1), pltpu.roll(order, 1, 1)
        )
        order = jnp.where(lane < bucket, swapped, order)[0:1, :]
        back = (row_id == order).astype(jnp.float32).astype(jnp.bfloat16)
        keys = jnp.dot(back, recv_buf[j, :, :width], preferred_element_type=jnp.float32)
        partner_vals[j] = jnp.dot(
            back, recv_buf[j, :, width:], preferred_element_type=jnp.float32
        )
        terms = keys * (q_vmem[...].astype(jnp.float32) * scale)
        score = jnp.zeros((heads, rows), jnp.float32)
        for term in split(terms):
            score = score + lax.dot_general(
                in_head, term, (((1,), (1,)), ((), ())), preferred_element_type=jnp.float32
            )
        for h in range(heads):
            score = score + jnp.where(bias_row == h, bias_ref[j, h], 0.0)
        expander_e[j] = score

    early = jnp.where(lax.rem(place, 2) == 0, 3, 2)

    at_edge = jnp.logical_or(at_first, at_last)
    far_soon = at_edge
    expander_step = (4, jnp.where(at_edge, 4, 6), jnp.where(at_edge, 5, 7))

    @pl.loop(0, 8)
    def _(step):
        @pl.when(jnp.logical_and(step == 3, jnp.logical_not(passes_end)))
        def _():
            far_tile(begin)

        for j in range(matchings):

            @pl.when(step == expander_step[j])
            def _():
                expander(j)

        @pl.when(step < 7)
        def _():
            late = jnp.where(far_soon, jnp.where(step == 4, 6, step - 1), step)
            late = jnp.where(jnp.logical_and(far_soon, step < 4), step, late)
            slot = jnp.where(
                step < 2,
                step,
                jnp.where(
                    step == 2,
                    early,
                    jnp.where(
                        step == 3,
                        early + 2,
                        jnp.where(late == 4, 5 - early, jnp.where(late == 5, 7 - early, 6)),
                    ),
                ),
            )

            for part in (1, 0):

                @pl.when(step > 0)
                def _():
                    tile_copy(0, slot, sibling, 1, part).wait_recv()

                for near in (2, 3):

                    @pl.when(slot == near)
                    def _():
                        passed_on(near, part, begin)

            offset = jnp.where(
                slot < 2,
                slot * (1 - 2 * core),
                jnp.where(
                    slot == 2,
                    -2,
                    jnp.where(
                        slot == 3,
                        2,
                        jnp.where(
                            slot == 4,
                            -1 - 2 * core,
                            jnp.where(slot == 5, 3 - 2 * core, 6 * core - 3),
                        ),
                    ),
                ),
            )
            absorb(slot, offset)

    acc_rows[...] = jnp.transpose(run_acc[...])


    top = run_max[...]
    for j in range(matchings):
        top = jnp.maximum(top, expander_e[j])
    block_part = jnp.exp(run_max[...] - top)
    weights = [jnp.exp(expander_e[j] - top) for j in range(matchings)]
    total = run_sum[...] * block_part
    for weight in weights:
        total = total + weight

    def spread(x):
        both = jnp.concatenate(split(x), axis=0)
        twice = jnp.concatenate([in_head, in_head], axis=0)
        return lax.dot_general(
            both, twice, (((0,), (0,)), ((), ())), preferred_element_type=jnp.float32
        )

    inverse = 1.0 / total
    attended = spread(block_part * inverse) * acc_rows[...]
    for j, weight in enumerate(weights):
        weight = weight.astype(jnp.bfloat16).astype(jnp.float32)
        attended = attended + spread(weight * inverse) * partner_vals[j]
    att_ref[...] = attended.astype(jnp.bfloat16)

    own_tiles(sent)
    far_tile(sent)
    for near in (2, 3):
        for part in range(2):
            passed_on(near, part, sent)
    for j in range(matchings):
        for b in BUCKET_ORDER:
            exp_copy(j, b).wait_send()


def solution(mesh):
    n_loop, n_grp = mesh.shape["loop"], mesh.shape["grp"]

    def shards(queries, key_rows, value_rows, out_weight, tile_list, order, bias):
        rows, width = queries.shape
        matchings, heads = bias.shape
        head = width // heads
        hbm = pl.BlockSpec(memory_space=pltpu.MemorySpace.HBM)
        vmem = pl.BlockSpec(memory_space=pltpu.VMEM)

        def body(*refs):
            kernel((n_loop, n_grp, matchings, heads, head), *refs)

        attended = pl.pallas_call(
            body,
            out_shape=jax.ShapeDtypeStruct((rows, width), jnp.bfloat16),
            in_specs=[hbm] * 6,
            out_specs=vmem,
            scratch_shapes=[
                pltpu.VMEM(order.shape, order.dtype),
                pltpu.SMEM(tile_list.shape, tile_list.dtype),
                pltpu.SMEM(bias.shape, bias.dtype),
                pltpu.VMEM((7, 2, rows, width), jnp.bfloat16),
                pltpu.VMEM((rows, width), jnp.bfloat16),
                pltpu.VMEM((heads // 2, 2 * head, 2 * rows), jnp.bfloat16),
                pltpu.VMEM((matchings, rows, 2 * width), jnp.bfloat16),
                pltpu.VMEM((matchings, rows, 2 * width), jnp.bfloat16),
                pltpu.VMEM((heads, rows), jnp.float32),
                pltpu.VMEM((heads, rows), jnp.float32),
                pltpu.VMEM((width, rows), jnp.float32),
                pltpu.VMEM((rows, width), jnp.float32),
                pltpu.VMEM((matchings, rows, width), jnp.float32),
                pltpu.VMEM((matchings, heads, rows), jnp.float32),
                pltpu.SemaphoreType.DMA((6,)),
                pltpu.SemaphoreType.DMA((8, 2)),
                pltpu.SemaphoreType.DMA((7, 2)),
                pltpu.SemaphoreType.DMA((matchings, n_grp)),
                pltpu.SemaphoreType.DMA((matchings, n_grp)),
            ],
            compiler_params=pltpu.CompilerParams(
                collective_id=0, has_side_effects=True, vmem_limit_bytes=40 * 2**20
            ),
        )(
            *(
                pltpu.with_memory_space_constraint(x, pltpu.MemorySpace.HBM)
                for x in (queries, key_rows, value_rows, order, tile_list, bias)
            )
        )
        return jnp.dot(attended, out_weight, preferred_element_type=jnp.float32).astype(
            jnp.bfloat16
        )

    rows_spec = P(("loop", "grp"), None)
    return jax.shard_map(
        shards,
        mesh=mesh,
        in_specs=(rows_spec, rows_spec, rows_spec, P(), rows_spec, P(None, ("loop", "grp")), P()),
        out_specs=rows_spec,
        check_vma=False,
    )
```
